32 devices in a mesh: groups: 2 (over x), seq: 16 (over z, y, core).
Axes of the slice: x: 2, y: 2, z: 4, core: 2. Of those that a mesh axis runs over, the one named last changes fastest.
Arguments:
- latent: bfloat16 [32, 32768], P(('groups', 'seq')), parts along dimension 0, may hold values from -6 to 6
- text_embed: bfloat16 [4, 128, 3072], P('groups'), parts along dimension 0, may hold values from -6 to 6
- text_mask: int32 [4, 128], P('groups'), parts along dimension 0, may hold values from 0 to 1, as said below
- modulation: float32 [4, 5, 3072], P('groups'), parts along dimension 0, may hold values from -3 to 10
- w_in: bfloat16 [64, 3072], replicated, may hold values from -0.75 to 0.75
- w_qkv: bfloat16 [3072, 4608], P(None, 'seq'), may hold values from -0.109375 to 0.109375
- w_attn_out: bfloat16 [1536, 3072], P(None, 'seq'), may hold values from -0.15625 to 0.15625
- w_final: bfloat16 [3072, 64], replicated, may hold values from -0.109375 to 0.109375
Outputs:
- guided: float32 [32, 32768], P(('groups', 'seq')), parts along dimension 0
The draws below stay inside these ranges and needn't reach their ends.
There are 2 independent parts, one for each index of `groups`. The reference program is written for one: setup_inputs(seed, part) draws one part's arguments, and reference() takes and returns one part's arrays. A program takes and returns all parts, laid end to end along the dimension named above; an argument that names none is the same for every part. Nothing has to cross between parts.
Inputs may be any that keep to these rules, and one draw needn't show every extreme that they name: `text_mask`: each row is 1 on a leading run of 1 to 127 positions and 0 after it.
All inputs are finite; a program needn't handle non-finite values.
Results may differ from the reference program's by a relative error of at most 0.007.
The reference program's roundings to bfloat16 on the way count: a program that leaves them out, or rounds other values in their place, can miss the bound.
Values may be sent and summed in bfloat16 or wider, within the bound.
A program may use at most 128 MiB of HBM per device.

```python
import jax
import jax.numpy as jnp
from jax import lax

D = 3072
HDIM = 128
SHEADS = 6
THEADS = 6
CHAN = 64
POS = 512
TXT = 128
HEADS = 12
FRAMES = 16
HALF = 8


def draw_text_mask(key, part):
    lengths = jax.random.randint(jax.random.fold_in(key, 7), (2, 1), 1, TXT)
    places = jnp.arange(TXT, dtype=jnp.int32)[None, :]
    return (places < lengths).astype(jnp.int32)


def draw_modulation(key, part):
    base = jnp.clip(0.5 * jax.random.normal(jax.random.fold_in(key, 11), (2, 5, D), jnp.float32), -3.0, 3.0)
    return base


def block_levels(key, dims, split, smallest, top_value):
    def one(dim, shards_of):
        steps = jax.random.uniform(jax.random.fold_in(jax.random.fold_in(key, 6), dim), (shards_of,), jnp.float32, smallest / len(split), top_value / len(split))
        return jnp.repeat(jnp.exp(steps), dims[dim] // shards_of).reshape((-1,) + (1,) * (len(dims) - dim - 1))

    factor_of = one(*split[0])
    for cut in split[1:]:
        factor_of = factor_of * one(*cut)
    return factor_of


def scatter_about(own_key, extent, width, reach, pieces=(), held_as=jnp.bfloat16):
    entries = width * jax.random.normal(own_key, extent, jnp.float32)
    if pieces:
        entries = entries * block_levels(own_key, extent, pieces, -0.22, 0.18)
    return jnp.clip(entries, -reach, reach).astype(held_as)


def setup_inputs(seed: int = 0, part: int = 0) -> dict:
    key_list = jax.random.split(jax.random.key(seed), 9)
    part_keys = jax.random.split(jax.random.fold_in(key_list[8], part), 9)
    latent = scatter_about(part_keys[0], (FRAMES, POS * CHAN), 1.0, 6.0, ((0, 16),))
    text_embed = scatter_about(part_keys[1], (2, TXT, D), 1.0, 6.0)
    text_mask = draw_text_mask(jax.random.fold_in(jax.random.fold_in(key_list[8], part), 71), part)
    modulation = draw_modulation(jax.random.fold_in(jax.random.fold_in(key_list[8], part), 71), part)
    w_in = scatter_about(key_list[4], (CHAN, D), CHAN ** -0.5, 0.75)
    w_qkv = scatter_about(key_list[5], (D, 3 * HEADS * HDIM), D ** -0.5, 0.109375, ((1, 16),))
    w_attn_out = scatter_about(key_list[6], (HEADS * HDIM, D), (HEADS * HDIM) ** -0.5, 0.15625, ((1, 16),))
    w_final = scatter_about(key_list[7], (D, CHAN), D ** -0.5, 0.109375)
    return {"latent": latent, "text_embed": text_embed, "text_mask": text_mask, "modulation": modulation, "w_in": w_in, "w_qkv": w_qkv, "w_attn_out": w_attn_out, "w_final": w_final}


EPS = 1e-06
GUIDE = 5.0

def normalize(values):
    center = values - lax.optimization_barrier(jnp.mean(values, axis=-1, keepdims=True))
    spread = lax.optimization_barrier(jnp.mean(center * center, axis=-1, keepdims=True))
    return center * lax.rsqrt(spread + EPS)

def attend(query, keys, values, live):
    scores = jnp.einsum('qhe,khe->hqk', query.astype(jnp.float32), keys.astype(jnp.float32)) * HDIM ** (-0.5)
    scores = jnp.where(live[None, None, :], scores, -1e+30)
    top = lax.optimization_barrier(jnp.max(scores, axis=-1, keepdims=True))
    weights = jnp.exp(scores - top)
    total = lax.optimization_barrier(jnp.sum(weights, axis=-1, keepdims=True))
    probs = weights.astype(jnp.bfloat16)
    mixed = jnp.einsum('hqk,khe->qhe', probs.astype(jnp.float32), values.astype(jnp.float32))
    return (mixed / jnp.transpose(total, (1, 0, 2))).astype(jnp.bfloat16)

def temporal_mix(block):
    frames, span, heads = (block.shape[0], block.shape[1], block.shape[3])
    grid = block.reshape(2, frames // 2, span, 3, heads, HDIM).astype(jnp.float32)
    scores = jnp.einsum('afpne,agpne->apnfg', grid[:, :, :, 0], grid[:, :, :, 1]) * HDIM ** (-0.5)
    top = lax.optimization_barrier(jnp.max(scores, axis=-1, keepdims=True))
    weights = jnp.exp(scores - top)
    total = lax.optimization_barrier(jnp.sum(weights, axis=-1))
    probs = weights.astype(jnp.bfloat16)
    mixed = jnp.einsum('apnfg,agpne->afpne', probs.astype(jnp.float32), grid[:, :, :, 2])
    mixed = mixed / jnp.moveaxis(total, 3, 1)[..., None]
    return mixed.astype(jnp.bfloat16).reshape(frames, span, heads, HDIM)

def reference(latent, text_embed, text_mask, modulation, w_in, w_qkv, w_attn_out, w_final):
    halves = (jnp.arange(FRAMES) // HALF).astype(jnp.int32)

    def spatial(item):
        row, half = item
        start = jnp.dot(row.reshape(POS, CHAN), w_in, preferred_element_type=jnp.float32)
        mods = modulation[half]
        hidden = (normalize(start) * (1.0 + mods[1]) + mods[0]).astype(jnp.bfloat16)
        rows = jnp.concatenate([hidden, text_embed[half]], axis=0)
        projected = jnp.dot(rows, w_qkv, preferred_element_type=jnp.float32).astype(jnp.bfloat16)
        projected = projected.reshape(POS + TXT, 3, HEADS, HDIM)
        live = jnp.concatenate([jnp.ones((POS,), bool), text_mask[half] > 0])
        spatial_out = attend(projected[:POS, 0, :SHEADS], projected[:, 1, :SHEADS], projected[:, 2, :SHEADS], live)
        return (start, spatial_out, projected[:POS, :, SHEADS:])
    starts, spatial_outs, temporal_in = lax.map(spatial, (latent, halves))
    temporal_outs = temporal_mix(temporal_in)

    def finish(item):
        start, spatial_out, temporal_out, half = item
        mods = modulation[half]
        joined = jnp.concatenate([spatial_out.reshape(POS, SHEADS * HDIM), temporal_out.reshape(POS, THEADS * HDIM)], axis=1)
        block = start + mods[2] * jnp.dot(joined, w_attn_out, preferred_element_type=jnp.float32)
        final = (normalize(block) * (1.0 + mods[4]) + mods[3]).astype(jnp.bfloat16)
        return jnp.dot(final, w_final, preferred_element_type=jnp.float32).astype(jnp.bfloat16)
    preds = lax.map(finish, (starts, spatial_outs, temporal_outs, halves)).astype(jnp.float32)
    cond_pred = preds[:HALF]
    uncond_pred = preds[HALF:]
    mixed = uncond_pred + GUIDE * (cond_pred - uncond_pred)
    return jnp.concatenate([mixed, mixed], axis=0).reshape(FRAMES, POS * CHAN)
```

```python
import jax
import jax.numpy as jnp
from jax import lax
from jax.sharding import PartitionSpec as P

HDIM = 128
SHEADS = 6
THEADS = 6
CHAN = 64
HEADS = 12


EPS = 1e-06
GUIDE = 5.0
QKV_CHUNKS = 2
OUT_CHUNKS = 1


def normalize(values):
    center = values - jnp.mean(values, axis=-1, keepdims=True)
    spread = jnp.mean(center * center, axis=-1, keepdims=True)
    return center * lax.rsqrt(spread + EPS)


def attend(query, keys, values, live):
    scores = jnp.einsum("qhe,khe->hqk", query, keys, preferred_element_type=jnp.float32) * HDIM ** (
        -0.5
    )
    scores = jnp.where(live[None, None, :], scores, -1e30)
    top = jnp.max(scores, axis=-1, keepdims=True)
    weights = jnp.exp(scores - top)
    total = jnp.sum(weights, axis=-1, keepdims=True)
    probs = weights.astype(jnp.bfloat16)
    mixed = jnp.einsum("hqk,khe->qhe", probs, values, preferred_element_type=jnp.float32)
    return (mixed / jnp.transpose(total, (1, 0, 2))).astype(jnp.bfloat16)


def temporal_mix(query, keys, values):
    frames, span = query.shape[0], query.shape[1]
    halved = (2, frames // 2, span, THEADS, HDIM)
    query, keys, values = (x.reshape(halved) for x in (query, keys, values))
    scores = jnp.einsum(
        "afpne,agpne->apnfg", query, keys, preferred_element_type=jnp.float32
    ) * HDIM ** (-0.5)
    top = jnp.max(scores, axis=-1, keepdims=True)
    weights = jnp.exp(scores - top)
    total = jnp.sum(weights, axis=-1)
    probs = weights.astype(jnp.bfloat16)
    mixed = jnp.einsum("apnfg,agpne->afpne", probs, values, preferred_element_type=jnp.float32)
    mixed = mixed / jnp.moveaxis(total, 3, 1)[..., None]
    return mixed.astype(jnp.bfloat16).reshape(frames, span, THEADS * HDIM)


def gather_chunks(weight, chunks):
    teams = lax.axis_size("groups")
    team = lax.axis_index("groups")
    flat = weight.T
    depth = flat.shape[1]
    piece = depth // (chunks * teams)
    pieces = []
    for chunk in range(chunks):
        mine = lax.dynamic_slice_in_dim(flat, (chunk * teams + team) * piece, piece, axis=1)
        whole = lax.all_gather(mine, ("groups", "seq"), axis=0, tiled=True)
        whole = whole.reshape(teams, -1, piece)
        for peer in range(teams):
            pieces.append(((chunk * teams + peer) * piece, whole[peer]))
    return pieces


def multiply(rows, pieces, first, width):
    total = None
    for offset, piece in pieces:
        part = lax.dot_general(
            rows[:, offset : offset + piece.shape[1]],
            piece[first : first + width],
            (((1,), (1,)), ((), ())),
            preferred_element_type=jnp.float32,
        )
        total = part if total is None else total + part
    return total


def per_device(latent, text_embed, text_mask, modulation, w_in, w_qkv, w_attn_out, w_final):
    count = lax.axis_size("seq")
    index = lax.axis_index("seq")
    half = index // (count // 2)
    positions = latent.shape[1] // CHAN
    span = positions // count
    latent_rows = latent.reshape(count, span, CHAN)
    latent_pos = lax.all_to_all(
        latent.reshape(1, count, span, CHAN), "seq", split_axis=1, concat_axis=0, tiled=True
    )
    qkv_pieces = gather_chunks(w_qkv, QKV_CHUNKS)
    out_pieces = gather_chunks(w_attn_out, OUT_CHUNKS)

    start = jnp.dot(latent_rows.reshape(positions, CHAN), w_in, preferred_element_type=jnp.float32)
    mods = lax.dynamic_index_in_dim(modulation, half, 0, keepdims=False)
    hidden = (normalize(start) * (1.0 + mods[1]) + mods[0]).astype(jnp.bfloat16)
    words = lax.dynamic_index_in_dim(text_embed, half, 0, keepdims=False)
    valid = lax.dynamic_index_in_dim(text_mask, half, 0, keepdims=False) > 0
    rows = jnp.concatenate([hidden, words], axis=0)

    cond_side = (jnp.arange(count) < count // 2)[:, None, None]
    frame_mods = jnp.where(cond_side, modulation[0][None], modulation[1][None])
    start_here = jnp.dot(
        latent_pos.reshape(positions, CHAN), w_in, preferred_element_type=jnp.float32
    ).reshape(count, span, -1)
    hidden_here = (
        normalize(start_here) * (1.0 + frame_mods[:, 1][:, None, :]) + frame_mods[:, 0][:, None, :]
    ).astype(jnp.bfloat16).reshape(positions, -1)

    swide, twide = SHEADS * HDIM, THEADS * HDIM
    spatial = [
        multiply(rows if i else hidden, qkv_pieces, i * HEADS * HDIM, swide)
        .astype(jnp.bfloat16)
        .reshape(-1, SHEADS, HDIM)
        for i in range(3)
    ]
    live = jnp.concatenate([jnp.ones((positions,), bool), valid])
    spatial_out = attend(spatial[0], spatial[1], spatial[2], live)
    spatial_pos = lax.all_to_all(
        spatial_out.reshape(1, count, span, swide), "seq", split_axis=1, concat_axis=0, tiled=True
    )
    temporal = [
        multiply(hidden_here, qkv_pieces, (i * HEADS + SHEADS) * HDIM, twide)
        .astype(jnp.bfloat16)
        .reshape(count, span, twide)
        for i in range(3)
    ]
    temporal_pos = temporal_mix(*temporal)
    joined = jnp.concatenate(
        [spatial_pos.reshape(positions, swide), temporal_pos.reshape(positions, twide)], axis=1
    )
    mixed_out = multiply(joined, out_pieces, 0, out_pieces[0][1].shape[0])
    block = start_here + frame_mods[:, 2][:, None, :] * mixed_out.reshape(count, span, -1)
    final = (
        normalize(block) * (1.0 + frame_mods[:, 4][:, None, :]) + frame_mods[:, 3][:, None, :]
    ).astype(jnp.bfloat16)
    pred = jnp.dot(
        final.reshape(positions, -1), w_final, preferred_element_type=jnp.float32
    ).astype(jnp.bfloat16)
    pred = lax.optimization_barrier(pred).astype(jnp.float32).reshape(count, span, CHAN)
    cond_pred = pred[: count // 2]
    uncond_pred = pred[count // 2 :]
    guided_here = uncond_pred + GUIDE * (cond_pred - uncond_pred)
    both_halves = jnp.concatenate([guided_here, guided_here], axis=0)
    result = lax.all_to_all(
        both_halves.astype(jnp.bfloat16), "seq", split_axis=0, concat_axis=1, tiled=True
    ).astype(both_halves.dtype)
    return result.reshape(1, positions * CHAN)


def solution(mesh):
    in_specs = (
        P(("groups", "seq"), None),
        P("groups", None, None),
        P("groups", None),
        P("groups", None, None),
        P(),
        P(None, "seq"),
        P(None, "seq"),
        P(),
    )
    out_specs = P(("groups", "seq"), None)
    return jax.shard_map(
        per_device, mesh=mesh, in_specs=in_specs, out_specs=out_specs, check_vma=False
    )
```

```python
import jax
import jax.numpy as jnp
from jax import lax
from jax.sharding import PartitionSpec as P

HDIM = 128
SHEADS = 6
THEADS = 6
CHAN = 64
HEADS = 12


EPS = 1e-06
GUIDE = 5.0
QKV_CHUNKS = 2
OUT_CHUNKS = 1


def normalize(values):
    center = values - jnp.mean(values, axis=-1, keepdims=True)
    spread = jnp.mean(center * center, axis=-1, keepdims=True)
    return center * lax.rsqrt(spread + EPS)


def attend(query, keys, values, live):
    scores = jnp.einsum("qhe,khe->hqk", query, keys, preferred_element_type=jnp.float32) * HDIM ** (
        -0.5
    )
    scores = jnp.where(live[None, None, :], scores, -1e30)
    top = jnp.max(scores, axis=-1, keepdims=True)
    weights = jnp.exp(scores - top)
    total = jnp.sum(weights, axis=-1, keepdims=True)
    probs = weights.astype(jnp.bfloat16)
    mixed = jnp.einsum("hqk,khe->qhe", probs, values, preferred_element_type=jnp.float32)
    return (mixed / jnp.transpose(total, (1, 0, 2))).astype(jnp.bfloat16)


def temporal_mix(query, keys, values):
    frames, span = query.shape[0], query.shape[1]
    halved = (2, frames // 2, span, THEADS, HDIM)
    query, keys, values = (x.reshape(halved) for x in (query, keys, values))
    scores = jnp.einsum(
        "afpne,agpne->apnfg", query, keys, preferred_element_type=jnp.float32
    ) * HDIM ** (-0.5)
    top = jnp.max(scores, axis=-1, keepdims=True)
    weights = jnp.exp(scores - top)
    total = jnp.sum(weights, axis=-1)
    probs = weights.astype(jnp.bfloat16)
    mixed = jnp.einsum("apnfg,agpne->afpne", probs, values, preferred_element_type=jnp.float32)
    mixed = mixed / jnp.moveaxis(total, 3, 1)[..., None]
    return mixed.astype(jnp.bfloat16).reshape(frames, span, THEADS * HDIM)


def gather_chunks(weight, chunks):
    flat = weight.T
    piece = flat.shape[1] // chunks
    pieces = []
    for chunk in range(chunks):
        mine = flat[:, chunk * piece : (chunk + 1) * piece]
        pieces.append((chunk * piece, lax.all_gather(mine, "seq", axis=0, tiled=True)))
    return pieces


def multiply(rows, pieces, first, width):
    total = None
    for offset, piece in pieces:
        part = lax.dot_general(
            rows[:, offset : offset + piece.shape[1]],
            piece[first : first + width],
            (((1,), (1,)), ((), ())),
            preferred_element_type=jnp.float32,
        )
        total = part if total is None else total + part
    return total


def per_device(latent, text_embed, text_mask, modulation, w_in, w_qkv, w_attn_out, w_final):
    count = lax.axis_size("seq")
    index = lax.axis_index("seq")
    half = index // (count // 2)
    positions = latent.shape[1] // CHAN
    span = positions // count
    latent_rows = latent.reshape(count, span, CHAN)
    latent_pos = lax.all_to_all(
        latent.reshape(1, count, span, CHAN), "seq", split_axis=1, concat_axis=0, tiled=True
    )
    qkv_pieces = gather_chunks(w_qkv, QKV_CHUNKS)
    out_pieces = gather_chunks(w_attn_out, OUT_CHUNKS)

    start = jnp.dot(latent_rows.reshape(positions, CHAN), w_in, preferred_element_type=jnp.float32)
    mods = lax.dynamic_index_in_dim(modulation, half, 0, keepdims=False)
    hidden = (normalize(start) * (1.0 + mods[1]) + mods[0]).astype(jnp.bfloat16)
    words = lax.dynamic_index_in_dim(text_embed, half, 0, keepdims=False)
    valid = lax.dynamic_index_in_dim(text_mask, half, 0, keepdims=False) > 0
    rows = jnp.concatenate([hidden, words], axis=0)

    cond_side = (jnp.arange(count) < count // 2)[:, None, None]
    frame_mods = jnp.where(cond_side, modulation[0][None], modulation[1][None])
    start_here = jnp.dot(
        latent_pos.reshape(positions, CHAN), w_in, preferred_element_type=jnp.float32
    ).reshape(count, span, -1)
    hidden_here = (
        normalize(start_here) * (1.0 + frame_mods[:, 1][:, None, :]) + frame_mods[:, 0][:, None, :]
    ).astype(jnp.bfloat16).reshape(positions, -1)

    swide, twide = SHEADS * HDIM, THEADS * HDIM
    spatial = [
        multiply(rows if i else hidden, qkv_pieces, i * HEADS * HDIM, swide)
        .astype(jnp.bfloat16)
        .reshape(-1, SHEADS, HDIM)
        for i in range(3)
    ]
    live = jnp.concatenate([jnp.ones((positions,), bool), valid])
    spatial_out = attend(spatial[0], spatial[1], spatial[2], live)
    spatial_pos = lax.all_to_all(
        spatial_out.reshape(1, count, span, swide), "seq", split_axis=1, concat_axis=0, tiled=True
    )
    temporal = [
        multiply(hidden_here, qkv_pieces, (i * HEADS + SHEADS) * HDIM, twide)
        .astype(jnp.bfloat16)
        .reshape(count, span, twide)
        for i in range(3)
    ]
    temporal_pos = temporal_mix(*temporal)
    joined = jnp.concatenate(
        [spatial_pos.reshape(positions, swide), temporal_pos.reshape(positions, twide)], axis=1
    )
    mixed_out = multiply(joined, out_pieces, 0, out_pieces[0][1].shape[0])
    block = start_here + frame_mods[:, 2][:, None, :] * mixed_out.reshape(count, span, -1)
    final = (
        normalize(block) * (1.0 + frame_mods[:, 4][:, None, :]) + frame_mods[:, 3][:, None, :]
    ).astype(jnp.bfloat16)
    pred = jnp.dot(
        final.reshape(positions, -1), w_final, preferred_element_type=jnp.float32
    ).astype(jnp.bfloat16)
    pred = lax.optimization_barrier(pred).astype(jnp.float32).reshape(count, span, CHAN)
    cond_pred = pred[: count // 2]
    uncond_pred = pred[count // 2 :]
    guided_here = uncond_pred + GUIDE * (cond_pred - uncond_pred)
    both_halves = jnp.concatenate([guided_here, guided_here], axis=0)
    result = lax.all_to_all(
        both_halves.astype(jnp.bfloat16), "seq", split_axis=0, concat_axis=1, tiled=True
    ).astype(both_halves.dtype)
    return result.reshape(1, positions * CHAN)


def solution(mesh):
    in_specs = (
        P(("groups", "seq"), None),
        P("groups", None, None),
        P("groups", None),
        P("groups", None, None),
        P(),
        P(None, "seq"),
        P(None, "seq"),
        P(),
    )
    out_specs = P(("groups", "seq"), None)
    return jax.shard_map(
        per_device, mesh=mesh, in_specs=in_specs, out_specs=out_specs, check_vma=False
    )
```

```python
import functools

import jax
import jax.numpy as jnp
from jax import lax
from jax.experimental import pallas as pl
from jax.experimental.pallas import tpu as pltpu
from jax.sharding import PartitionSpec as P

HDIM = 128
SHEADS = 6
THEADS = 6
CHAN = 64
HEADS = 12


EPS = 1e-06
GUIDE = 5.0


def normalize(values):
    center = values - jnp.mean(values, axis=-1, keepdims=True)
    spread = jnp.mean(center * center, axis=-1, keepdims=True)
    return center * lax.rsqrt(spread + EPS)


def attend(query, keys, values, live):
    scores = jnp.einsum("qhe,khe->hqk", query, keys, preferred_element_type=jnp.float32) * HDIM ** (
        -0.5
    )
    scores = jnp.where(live[None, None, :], scores, -1e30)
    top = jnp.max(scores, axis=-1, keepdims=True)
    weights = jnp.exp(scores - top)
    total = jnp.sum(weights, axis=-1, keepdims=True)
    probs = weights.astype(jnp.bfloat16)
    mixed = jnp.einsum("hqk,khe->qhe", probs, values, preferred_element_type=jnp.float32)
    return (mixed / jnp.transpose(total, (1, 0, 2))).astype(jnp.bfloat16)


def temporal_mix(query, keys, values):
    frames, span = query.shape[0], query.shape[1]
    halved = (2, frames // 2, span, THEADS, HDIM)
    query, keys, values = (x.reshape(halved) for x in (query, keys, values))
    scores = jnp.einsum(
        "afpne,agpne->apnfg", query, keys, preferred_element_type=jnp.float32
    ) * HDIM ** (-0.5)
    top = jnp.max(scores, axis=-1, keepdims=True)
    weights = jnp.exp(scores - top)
    total = jnp.sum(weights, axis=-1)
    probs = weights.astype(jnp.bfloat16)
    mixed = jnp.einsum("apnfg,agpne->afpne", probs, values, preferred_element_type=jnp.float32)
    mixed = mixed / jnp.moveaxis(total, 3, 1)[..., None]
    return mixed.astype(jnp.bfloat16).reshape(frames, span, THEADS * HDIM)


def gather_kernel(count, weight, whole, own_sem, ring_send, ring_recv, x_send, x_recv, core_send, core_recv):
    chips = count // 2
    team, me = lax.axis_index("groups"), lax.axis_index("seq")
    core, chip = me % 2, me // 2
    third = weight.shape[0] // 3
    place = (1 - chip % 2) * (chip // 2) + (chip % 2) * (chips - 1 - chip // 2)
    right_third, left_third = 2 * (team % 2), 1
    x_third = 2 - right_third

    def shard(spot):
        spot = (spot + 2 * chips) % chips
        late = spot // (chips // 2)
        return 2 * ((1 - late) * 2 * spot + late * (2 * (chips - 1 - spot) + 1)) + core

    def rows(part):
        return pl.ds(pl.multiple_of(part * third, third), third)

    right, left = {"seq": shard(place + 1)}, {"seq": shard(place - 1)}
    sibling = {"seq": chip * 2 + 1 - core}
    across = {"groups": team + 1 - 2 * (team % 2)}

    barrier = pltpu.get_barrier_semaphore()
    for peer in (right, left, sibling, across):
        pl.semaphore_signal(barrier, inc=1, device_id=peer, device_id_type=pl.DeviceIdType.MESH)
    pl.semaphore_wait(barrier, 4)

    def remote(src, dst, send, recv, peer):
        return pltpu.make_async_remote_copy(
            src_ref=src,
            dst_ref=dst,
            send_sem=send,
            recv_sem=recv,
            device_id=peer,
            device_id_type=pl.DeviceIdType.MESH,
        )

    def piece(spot, part):
        return whole.at[shard(spot), rows(part)]

    def ring(way, step, sending):
        toward = (1, -1)[way]
        part = (right_third, left_third)[way]
        spot = place - toward * step if sending else place - toward * (step + 1)
        view = piece(spot, part)
        src = weight.at[rows(part)] if sending and step == 0 else view
        return remote(src, view, ring_send.at[way, step], ring_recv.at[way, step], (right, left)[way])

    def cross(step, sending):
        view = piece(place - step - 1, right_third if sending else x_third)
        return remote(view, view, x_send.at[step], x_recv.at[step], across)

    def twin(kind, step, sending):
        spot = (place - step - 1, place + step + 1, place - step - 1)[kind]
        view = piece(spot, (right_third, left_third, x_third)[kind])
        if not sending:
            other = chip_shard(spot)
            view = whole.at[other, rows((right_third, left_third, x_third)[kind])]
        return remote(view, view, core_send.at[kind, step], core_recv.at[kind, step], sibling)

    def chip_shard(spot):
        return shard(spot) + 1 - 2 * core

    own = pltpu.make_async_copy(weight, whole.at[me], own_sem.at[0])
    lent = remote(weight, whole.at[me], own_sem.at[1], own_sem.at[2], sibling)
    borrowed = remote(weight, whole.at[chip * 2 + 1 - core], own_sem.at[1], own_sem.at[2], sibling)
    steps = chips - 1
    ring(0, 0, True).start()
    ring(1, 0, True).start()
    own.start()
    lent.start()
    for step in range(steps):
        for way in range(2):
            ring(way, step, False).wait_recv()
            if step + 1 < steps:
                ring(way, step + 1, True).start()
            if way == 0:
                cross(step, True).start()
            twin(way, step, True).start()
        if step:
            cross(step - 1, False).wait_recv()
            twin(2, step - 1, True).start()
    cross(steps - 1, False).wait_recv()
    twin(2, steps - 1, True).start()
    for step in range(steps):
        for way in range(2):
            ring(way, step, True).wait_send()
        cross(step, True).wait_send()
        for kind in range(3):
            twin(kind, step, True).wait_send()
            twin(kind, step, False).wait_recv()
    own.wait()
    lent.wait_send()
    borrowed.wait_recv()


def gather_weight(weight):
    count = lax.axis_size("seq")
    steps = count // 2 - 1
    whole = pl.pallas_call(
        functools.partial(gather_kernel, count),
        out_shape=jax.ShapeDtypeStruct((count,) + weight.shape, weight.dtype),
        in_specs=[pl.BlockSpec(memory_space=pl.ANY)],
        out_specs=pl.BlockSpec(memory_space=pl.ANY),
        scratch_shapes=[
            pltpu.SemaphoreType.DMA((3,)),
            pltpu.SemaphoreType.DMA((2, steps)),
            pltpu.SemaphoreType.DMA((2, steps)),
            pltpu.SemaphoreType.DMA((steps,)),
            pltpu.SemaphoreType.DMA((steps,)),
            pltpu.SemaphoreType.DMA((3, steps)),
            pltpu.SemaphoreType.DMA((3, steps)),
        ],
        compiler_params=pltpu.CompilerParams(collective_id=0, has_side_effects=True),
    )(weight)
    return whole.reshape(count * weight.shape[0], weight.shape[1])


def multiply(rows, flat, first, width):
    return lax.dot_general(
        rows,
        flat[first : first + width],
        (((1,), (1,)), ((), ())),
        preferred_element_type=jnp.float32,
    )


def per_device(latent, text_embed, text_mask, modulation, w_in, w_qkv, w_attn_out, w_final):
    count = lax.axis_size("seq")
    index = lax.axis_index("seq")
    half = index // (count // 2)
    positions = latent.shape[1] // CHAN
    span = positions // count
    latent_rows = latent.reshape(count, span, CHAN)
    latent_pos = lax.all_to_all(
        latent.reshape(1, count, span, CHAN), "seq", split_axis=1, concat_axis=0, tiled=True
    )
    out_flat = lax.all_gather(w_attn_out.T, "seq", axis=0, tiled=True)
    qkv_flat = gather_weight(w_qkv.T)

    start = jnp.dot(latent_rows.reshape(positions, CHAN), w_in, preferred_element_type=jnp.float32)
    mods = lax.dynamic_index_in_dim(modulation, half, 0, keepdims=False)
    hidden = (normalize(start) * (1.0 + mods[1]) + mods[0]).astype(jnp.bfloat16)
    words = lax.dynamic_index_in_dim(text_embed, half, 0, keepdims=False)
    valid = lax.dynamic_index_in_dim(text_mask, half, 0, keepdims=False) > 0
    rows = jnp.concatenate([hidden, words], axis=0)

    cond_side = (jnp.arange(count) < count // 2)[:, None, None]
    frame_mods = jnp.where(cond_side, modulation[0][None], modulation[1][None])
    start_here = jnp.dot(
        latent_pos.reshape(positions, CHAN), w_in, preferred_element_type=jnp.float32
    ).reshape(count, span, -1)
    hidden_here = (
        normalize(start_here) * (1.0 + frame_mods[:, 1][:, None, :]) + frame_mods[:, 0][:, None, :]
    ).astype(jnp.bfloat16).reshape(positions, -1)

    swide, twide = SHEADS * HDIM, THEADS * HDIM
    spatial = [
        multiply(rows if i else hidden, qkv_flat, i * HEADS * HDIM, swide)
        .astype(jnp.bfloat16)
        .reshape(-1, SHEADS, HDIM)
        for i in range(3)
    ]
    live = jnp.concatenate([jnp.ones((positions,), bool), valid])
    spatial_out = attend(spatial[0], spatial[1], spatial[2], live)
    spatial_pos = lax.all_to_all(
        spatial_out.reshape(1, count, span, swide), "seq", split_axis=1, concat_axis=0, tiled=True
    )
    temporal = [
        multiply(hidden_here, qkv_flat, (i * HEADS + SHEADS) * HDIM, twide)
        .astype(jnp.bfloat16)
        .reshape(count, span, twide)
        for i in range(3)
    ]
    temporal_pos = temporal_mix(*temporal)
    joined = jnp.concatenate(
        [spatial_pos.reshape(positions, swide), temporal_pos.reshape(positions, twide)], axis=1
    )
    mixed_out = multiply(joined, out_flat, 0, out_flat.shape[0])
    block = start_here + frame_mods[:, 2][:, None, :] * mixed_out.reshape(count, span, -1)
    final = (
        normalize(block) * (1.0 + frame_mods[:, 4][:, None, :]) + frame_mods[:, 3][:, None, :]
    ).astype(jnp.bfloat16)
    pred = jnp.dot(
        final.reshape(positions, -1), w_final, preferred_element_type=jnp.float32
    ).astype(jnp.bfloat16)
    pred = lax.optimization_barrier(pred).astype(jnp.float32).reshape(count, span, CHAN)
    cond_pred = pred[: count // 2]
    uncond_pred = pred[count // 2 :]
    guided_here = uncond_pred + GUIDE * (cond_pred - uncond_pred)
    both_halves = jnp.concatenate([guided_here, guided_here], axis=0)
    result = lax.all_to_all(
        both_halves.astype(jnp.bfloat16), "seq", split_axis=0, concat_axis=1, tiled=True
    ).astype(both_halves.dtype)
    return result.reshape(1, positions * CHAN)


def solution(mesh):
    in_specs = (
        P(("groups", "seq"), None),
        P("groups", None, None),
        P("groups", None),
        P("groups", None, None),
        P(),
        P(None, "seq"),
        P(None, "seq"),
        P(),
    )
    out_specs = P(("groups", "seq"), None)
    return jax.shard_map(
        per_device, mesh=mesh, in_specs=in_specs, out_specs=out_specs, check_vma=False
    )
```

```python
import functools

import jax
import jax.numpy as jnp
from jax import lax
from jax.experimental import pallas as pl
from jax.experimental.pallas import tpu as pltpu
from jax.sharding import PartitionSpec as P

HDIM = 128
SHEADS = 6
THEADS = 6
CHAN = 64
HEADS = 12


EPS = 1e-06
GUIDE = 5.0


def normalize(values):
    center = values - jnp.mean(values, axis=-1, keepdims=True)
    spread = jnp.mean(center * center, axis=-1, keepdims=True)
    return center * lax.rsqrt(spread + EPS)


def attend_kernel(query, keys, values, live, out):
    scores = lax.dot_general(
        query[...], keys[...], (((1,), (1,)), ((), ())), preferred_element_type=jnp.float32
    ) * HDIM ** (-0.5)
    scores = jnp.where(live[...] > 0, scores, -1e30)
    top = jnp.max(scores, axis=-1, keepdims=True)
    weights = jnp.exp(scores - top)
    total = jnp.sum(weights, axis=-1, keepdims=True)
    mixed = jnp.dot(
        weights.astype(jnp.bfloat16), values[...], preferred_element_type=jnp.float32
    )
    out[...] = (mixed / total).astype(jnp.bfloat16)


def attend(query, keys, values, live):
    def column(rows):
        return pl.BlockSpec((rows, HDIM), lambda head: (0, head))

    return pl.pallas_call(
        attend_kernel,
        grid=(query.shape[1] // HDIM,),
        out_shape=jax.ShapeDtypeStruct(query.shape, jnp.bfloat16),
        in_specs=[
            column(query.shape[0]),
            column(keys.shape[0]),
            column(keys.shape[0]),
            pl.BlockSpec(live.shape, lambda head: (0, 0)),
        ],
        out_specs=column(query.shape[0]),
    )(query, keys, values, live)


def temporal_mix(query, keys, values):
    frames, span = query.shape[0], query.shape[1]
    halved = (2, frames // 2, span, THEADS, HDIM)
    query, keys, values = (x.reshape(halved) for x in (query, keys, values))
    scores = jnp.einsum(
        "afpne,agpne->apnfg", query, keys, preferred_element_type=jnp.float32
    ) * HDIM ** (-0.5)
    top = jnp.max(scores, axis=-1, keepdims=True)
    weights = jnp.exp(scores - top)
    total = jnp.sum(weights, axis=-1)
    probs = weights.astype(jnp.bfloat16)
    mixed = jnp.einsum("apnfg,agpne->afpne", probs, values, preferred_element_type=jnp.float32)
    mixed = mixed / jnp.moveaxis(total, 3, 1)[..., None]
    return mixed.astype(jnp.bfloat16).reshape(frames, span, THEADS * HDIM)


def gather_kernel(count, number, *refs):
    weights, wholes = refs[:number], refs[number : 2 * number]
    own_sem, ring_send, ring_recv, x_send, x_recv, core_send, core_recv = refs[2 * number :]
    chips = count // 2
    team, me = lax.axis_index("groups"), lax.axis_index("seq")
    core, chip = me % 2, me // 2
    place = (1 - chip % 2) * (chip // 2) + (chip % 2) * (chips - 1 - chip // 2)
    right_third, left_third = 2 * (team % 2), 1
    x_third = 2 - right_third
    parts = (right_third, left_third, x_third)

    def shard(spot, lane):
        spot = (spot + 2 * chips) % chips
        late = spot // (chips // 2)
        return 2 * ((1 - late) * 2 * spot + late * (2 * (chips - 1 - spot) + 1)) + lane

    def rows(item, part):
        third = weights[item].shape[0] // 3
        return pl.ds(pl.multiple_of(part * third, third), third)

    right, left = {"seq": shard(place + 1, core)}, {"seq": shard(place - 1, core)}
    sibling = {"seq": chip * 2 + 1 - core}
    across = {"groups": team + 1 - 2 * (team % 2)}

    barrier = pltpu.get_barrier_semaphore()
    for peer in (right, left, sibling, across):
        pl.semaphore_signal(barrier, inc=1, device_id=peer, device_id_type=pl.DeviceIdType.MESH)
    pl.semaphore_wait(barrier, 4)

    def remote(src, dst, send, recv, peer):
        return pltpu.make_async_remote_copy(
            src_ref=src,
            dst_ref=dst,
            send_sem=send,
            recv_sem=recv,
            device_id=peer,
            device_id_type=pl.DeviceIdType.MESH,
        )

    def ring(item, way, step, sending):
        toward = (1, -1)[way]
        spot = place - toward * step if sending else place - toward * (step + 1)
        view = wholes[item].at[shard(spot, core), rows(item, parts[way])]
        src = weights[item].at[rows(item, parts[way])] if sending and step == 0 else view
        at = (item, way, step)
        return remote(src, view, ring_send.at[at], ring_recv.at[at], (right, left)[way])

    def cross(item, step, sending):
        part = right_third if sending else x_third
        view = wholes[item].at[shard(place - step - 1, core), rows(item, part)]
        return remote(view, view, x_send.at[item, step], x_recv.at[item, step], across)

    def twin(item, kind, step, sending):
        spot = (place - step - 1, place + step + 1, place - step - 1)[kind]
        lane = core if sending else 1 - core
        view = wholes[item].at[shard(spot, lane), rows(item, parts[kind])]
        at = (item, kind, step)
        return remote(view, view, core_send.at[at], core_recv.at[at], sibling)

    def lend(item, whose):
        view = wholes[item].at[whose]
        return remote(weights[item], view, own_sem.at[item, 1], own_sem.at[item, 2], sibling)

    items = range(number)
    steps = chips - 1
    own = [pltpu.make_async_copy(weights[i], wholes[i].at[me], own_sem.at[i, 0]) for i in items]
    for item in items:
        for way in range(2):
            ring(item, way, 0, True).start()
    for item in items:
        own[item].start()
        lend(item, me).start()
    for step in range(steps):
        for item in items:
            for way in range(2):
                ring(item, way, step, False).wait_recv()
                if step + 1 < steps:
                    ring(item, way, step + 1, True).start()
                if way == 0:
                    cross(item, step, True).start()
                twin(item, way, step, True).start()
            if step:
                cross(item, step - 1, False).wait_recv()
                twin(item, 2, step - 1, True).start()
    for item in items:
        cross(item, steps - 1, False).wait_recv()
        twin(item, 2, steps - 1, True).start()
    for item in items:
        for step in range(steps):
            for way in range(2):
                ring(item, way, step, True).wait_send()
            cross(item, step, True).wait_send()
            for kind in range(3):
                twin(item, kind, step, True).wait_send()
                twin(item, kind, step, False).wait_recv()
        own[item].wait()
        lend(item, me).wait_send()
        lend(item, chip * 2 + 1 - core).wait_recv()


def gather_weights(*weights):
    count = lax.axis_size("seq")
    number, steps = len(weights), count // 2 - 1
    wholes = pl.pallas_call(
        functools.partial(gather_kernel, count, number),
        out_shape=[jax.ShapeDtypeStruct((count,) + w.shape, w.dtype) for w in weights],
        in_specs=[pl.BlockSpec(memory_space=pl.ANY)] * number,
        out_specs=[pl.BlockSpec(memory_space=pl.ANY)] * number,
        scratch_shapes=[
            pltpu.SemaphoreType.DMA((number, 3)),
            pltpu.SemaphoreType.DMA((number, 2, steps)),
            pltpu.SemaphoreType.DMA((number, 2, steps)),
            pltpu.SemaphoreType.DMA((number, steps)),
            pltpu.SemaphoreType.DMA((number, steps)),
            pltpu.SemaphoreType.DMA((number, 3, steps)),
            pltpu.SemaphoreType.DMA((number, 3, steps)),
        ],
        compiler_params=pltpu.CompilerParams(collective_id=0, has_side_effects=True),
    )(*weights)
    return [x.reshape(count * w.shape[0], w.shape[1]) for x, w in zip(wholes, weights)]


def multiply(rows, flat, first, width):
    return lax.dot_general(
        rows,
        flat[first : first + width],
        (((1,), (1,)), ((), ())),
        preferred_element_type=jnp.float32,
    )


def per_device(latent, text_embed, text_mask, modulation, w_in, w_qkv, w_attn_out, w_final):
    count = lax.axis_size("seq")
    index = lax.axis_index("seq")
    half = index // (count // 2)
    positions = latent.shape[1] // CHAN
    span = positions // count
    latent_rows = latent.reshape(count, span, CHAN)
    latent_pos = lax.all_to_all(
        latent.reshape(1, count, span, CHAN), "seq", split_axis=1, concat_axis=0, tiled=True
    )
    qkv_flat, out_flat = gather_weights(w_qkv.T, w_attn_out.T)

    start = jnp.dot(latent_rows.reshape(positions, CHAN), w_in, preferred_element_type=jnp.float32)
    mods = lax.dynamic_index_in_dim(modulation, half, 0, keepdims=False)
    hidden = (normalize(start) * (1.0 + mods[1]) + mods[0]).astype(jnp.bfloat16)
    words = lax.dynamic_index_in_dim(text_embed, half, 0, keepdims=False)
    valid = lax.dynamic_index_in_dim(text_mask, half, 0, keepdims=False) > 0
    rows = jnp.concatenate([hidden, words], axis=0)

    cond_side = (jnp.arange(count) < count // 2)[:, None, None]
    frame_mods = jnp.where(cond_side, modulation[0][None], modulation[1][None])
    start_here = jnp.dot(
        latent_pos.reshape(positions, CHAN), w_in, preferred_element_type=jnp.float32
    ).reshape(count, span, -1)
    hidden_here = (
        normalize(start_here) * (1.0 + frame_mods[:, 1][:, None, :]) + frame_mods[:, 0][:, None, :]
    ).astype(jnp.bfloat16).reshape(positions, -1)

    swide, twide = SHEADS * HDIM, THEADS * HDIM
    spatial = [
        multiply(rows if i else hidden, qkv_flat, i * HEADS * HDIM, swide)
        .astype(jnp.bfloat16)
        for i in range(3)
    ]
    live = jnp.concatenate([jnp.ones((positions,), jnp.int32), valid.astype(jnp.int32)])[None]
    spatial_out = attend(spatial[0], spatial[1], spatial[2], live)
    spatial_pos = lax.all_to_all(
        spatial_out.reshape(1, count, span, swide), "seq", split_axis=1, concat_axis=0, tiled=True
    )
    temporal = [
        multiply(hidden_here, qkv_flat, (i * HEADS + SHEADS) * HDIM, twide)
        .astype(jnp.bfloat16)
        .reshape(count, span, twide)
        for i in range(3)
    ]
    temporal_pos = temporal_mix(*temporal)
    joined = jnp.concatenate(
        [spatial_pos.reshape(positions, swide), temporal_pos.reshape(positions, twide)], axis=1
    )
    mixed_out = multiply(joined, out_flat, 0, out_flat.shape[0])
    block = start_here + frame_mods[:, 2][:, None, :] * mixed_out.reshape(count, span, -1)
    final = (
        normalize(block) * (1.0 + frame_mods[:, 4][:, None, :]) + frame_mods[:, 3][:, None, :]
    ).astype(jnp.bfloat16)
    pred = jnp.dot(
        final.reshape(positions, -1), w_final, preferred_element_type=jnp.float32
    ).astype(jnp.bfloat16)
    pred = lax.optimization_barrier(pred).astype(jnp.float32).reshape(count, span, CHAN)
    cond_pred = pred[: count // 2]
    uncond_pred = pred[count // 2 :]
    guided_here = uncond_pred + GUIDE * (cond_pred - uncond_pred)
    both_halves = jnp.concatenate([guided_here, guided_here], axis=0)
    result = lax.all_to_all(
        both_halves.astype(jnp.bfloat16), "seq", split_axis=0, concat_axis=1, tiled=True
    ).astype(both_halves.dtype)
    return result.reshape(1, positions * CHAN)


def solution(mesh):
    in_specs = (
        P(("groups", "seq"), None),
        P("groups", None, None),
        P("groups", None),
        P("groups", None, None),
        P(),
        P(None, "seq"),
        P(None, "seq"),
        P(),
    )
    out_specs = P(("groups", "seq"), None)
    return jax.shard_map(
        per_device, mesh=mesh, in_specs=in_specs, out_specs=out_specs, check_vma=False
    )
```

```python
import functools

import jax
import jax.numpy as jnp
from jax import lax
from jax.experimental import pallas as pl
from jax.experimental.pallas import tpu as pltpu
from jax.sharding import PartitionSpec as P

HDIM = 128
SHEADS = 6
THEADS = 6
CHAN = 64
HEADS = 12


EPS = 1e-06
GUIDE = 5.0


def normalize(values):
    center = values - jnp.mean(values, axis=-1, keepdims=True)
    spread = jnp.mean(center * center, axis=-1, keepdims=True)
    return center * lax.rsqrt(spread + EPS)


def attend_kernel(query, keys, values, live, out):
    rows = query.shape[0]
    block = min(128, rows)
    for first in range(0, rows, block):
        at = pl.ds(first, block)
        scores = lax.dot_general(
            query[at, :], keys[...], (((1,), (1,)), ((), ())), preferred_element_type=jnp.float32
        ) * HDIM ** (-0.5)
        scores = jnp.where(live[...] > 0, scores, -1e30)
        top = jnp.max(scores, axis=-1, keepdims=True)
        weights = jnp.exp(scores - top)
        total = jnp.sum(weights, axis=-1, keepdims=True)
        mixed = jnp.dot(
            weights.astype(jnp.bfloat16), values[...], preferred_element_type=jnp.float32
        )
        out[at, :] = (mixed / total).astype(jnp.bfloat16)


def attend(query, keys, values, live):
    def column(rows):
        return pl.BlockSpec((rows, HDIM), lambda head: (0, head))

    return pl.pallas_call(
        attend_kernel,
        grid=(query.shape[1] // HDIM,),
        out_shape=jax.ShapeDtypeStruct(query.shape, jnp.bfloat16),
        in_specs=[
            column(query.shape[0]),
            column(keys.shape[0]),
            column(keys.shape[0]),
            pl.BlockSpec(live.shape, lambda head: (0, 0)),
        ],
        out_specs=column(query.shape[0]),
    )(query, keys, values, live)


def temporal_mix(query, keys, values):
    frames, span = query.shape[0], query.shape[1]
    halved = (2, frames // 2, span, THEADS, HDIM)
    query, keys, values = (x.reshape(halved) for x in (query, keys, values))
    scores = jnp.einsum(
        "afpne,agpne->apnfg", query, keys, preferred_element_type=jnp.float32
    ) * HDIM ** (-0.5)
    top = jnp.max(scores, axis=-1, keepdims=True)
    weights = jnp.exp(scores - top)
    total = jnp.sum(weights, axis=-1)
    probs = weights.astype(jnp.bfloat16)
    mixed = jnp.einsum("apnfg,agpne->afpne", probs, values, preferred_element_type=jnp.float32)
    mixed = mixed / jnp.moveaxis(total, 3, 1)[..., None]
    return mixed.astype(jnp.bfloat16).reshape(frames, span, THEADS * HDIM)


def load_list(weights):
    loads = []
    for which, weight in enumerate(weights):
        third = weight.shape[0] // 3
        cuts = max(c for c in (1, 2, 3) if third % (16 * c) == 0)
        loads += [(cut / cuts, which, cut, third // cuts) for cut in range(cuts)]
    return [load[1:] for load in sorted(loads)]


def gather_kernel(count, number, *refs):
    weights, wholes = refs[:number], refs[number : 2 * number]
    own_sem, ring_send, ring_recv, x_send, x_recv, core_send, core_recv = refs[2 * number :]
    chips = count // 2
    team, me = lax.axis_index("groups"), lax.axis_index("seq")
    core, chip = me % 2, me // 2
    place = (1 - chip % 2) * (chip // 2) + (chip % 2) * (chips - 1 - chip // 2)
    right_third, left_third = 2 * (team % 2), 1
    x_third = 2 - right_third
    parts = (right_third, left_third, x_third)

    def shard(spot, lane):
        spot = (spot + 2 * chips) % chips
        late = spot // (chips // 2)
        return 2 * ((1 - late) * 2 * spot + late * (2 * (chips - 1 - spot) + 1)) + lane

    loads = load_list(weights)

    def rows(item, part):
        which, cut, extent = loads[item]
        third = weights[which].shape[0] // 3
        return pl.ds(pl.multiple_of(part * third + cut * extent, extent), extent)

    def whole(item):
        return wholes[loads[item][0]]

    right, left = {"seq": shard(place + 1, core)}, {"seq": shard(place - 1, core)}
    sibling = {"seq": chip * 2 + 1 - core}
    across = {"groups": team + 1 - 2 * (team % 2)}

    barrier = pltpu.get_barrier_semaphore()
    for peer in (right, left, sibling, across):
        pl.semaphore_signal(barrier, inc=1, device_id=peer, device_id_type=pl.DeviceIdType.MESH)
    pl.semaphore_wait(barrier, 4)

    def remote(src, dst, send, recv, peer):
        return pltpu.make_async_remote_copy(
            src_ref=src,
            dst_ref=dst,
            send_sem=send,
            recv_sem=recv,
            device_id=peer,
            device_id_type=pl.DeviceIdType.MESH,
        )

    def ring(item, way, step, sending):
        toward = (1, -1)[way]
        spot = place - toward * step if sending else place - toward * (step + 1)
        view = whole(item).at[shard(spot, core), rows(item, parts[way])]
        src = weights[loads[item][0]].at[rows(item, parts[way])] if sending and step == 0 else view
        at = (item, way, step)
        return remote(src, view, ring_send.at[at], ring_recv.at[at], (right, left)[way])

    def cross(item, step, sending):
        part = right_third if sending else x_third
        view = whole(item).at[shard(place - step - 1, core), rows(item, part)]
        return remote(view, view, x_send.at[item, step], x_recv.at[item, step], across)

    def twin(item, kind, step, sending):
        spot = (place - step - 1, place + step + 1, place - step - 1)[kind]
        lane = core if sending else 1 - core
        view = whole(item).at[shard(spot, lane), rows(item, parts[kind])]
        at = (item, kind, step)
        return remote(view, view, core_send.at[at], core_recv.at[at], sibling)

    def lend(item, whose):
        view = wholes[item].at[whose]
        return remote(weights[item], view, own_sem.at[item, 1], own_sem.at[item, 2], sibling)

    items = range(len(loads))
    steps = chips - 1
    own = [pltpu.make_async_copy(weights[i], wholes[i].at[me], own_sem.at[i, 0]) for i in range(number)]
    for item in items:
        for way in range(2):
            ring(item, way, 0, True).start()
    for item in range(number):
        own[item].start()
        lend(item, me).start()
    for step in range(steps):
        for item in items:
            for way in range(2):
                ring(item, way, step, False).wait_recv()
                if step + 1 < steps:
                    ring(item, way, step + 1, True).start()
                if way == 0:
                    cross(item, step, True).start()
                twin(item, way, step, True).start()
            if step:
                cross(item, step - 1, False).wait_recv()
                twin(item, 2, step - 1, True).start()
    for item in items:
        cross(item, steps - 1, False).wait_recv()
        twin(item, 2, steps - 1, True).start()
    for item in items:
        for step in range(steps):
            for way in range(2):
                ring(item, way, step, True).wait_send()
            cross(item, step, True).wait_send()
            for kind in range(3):
                twin(item, kind, step, True).wait_send()
                twin(item, kind, step, False).wait_recv()
    for item in range(number):
        own[item].wait()
        lend(item, me).wait_send()
        lend(item, chip * 2 + 1 - core).wait_recv()


def gather_weights(*weights):
    count = lax.axis_size("seq")
    number, steps, loads = len(weights), count // 2 - 1, len(load_list(weights))
    wholes = pl.pallas_call(
        functools.partial(gather_kernel, count, number),
        out_shape=[jax.ShapeDtypeStruct((count,) + w.shape, w.dtype) for w in weights],
        in_specs=[pl.BlockSpec(memory_space=pl.ANY)] * number,
        out_specs=[pl.BlockSpec(memory_space=pl.ANY)] * number,
        scratch_shapes=[
            pltpu.SemaphoreType.DMA((number, 3)),
            pltpu.SemaphoreType.DMA((loads, 2, steps)),
            pltpu.SemaphoreType.DMA((loads, 2, steps)),
            pltpu.SemaphoreType.DMA((loads, steps)),
            pltpu.SemaphoreType.DMA((loads, steps)),
            pltpu.SemaphoreType.DMA((loads, 3, steps)),
            pltpu.SemaphoreType.DMA((loads, 3, steps)),
        ],
        compiler_params=pltpu.CompilerParams(collective_id=0, has_side_effects=True),
    )(*weights)
    return [x.reshape(count * w.shape[0], w.shape[1]) for x, w in zip(wholes, weights)]


def multiply(rows, flat, first, width):
    return lax.dot_general(
        rows,
        flat[first : first + width],
        (((1,), (1,)), ((), ())),
        preferred_element_type=jnp.float32,
    )


def per_device(latent, text_embed, text_mask, modulation, w_in, w_qkv, w_attn_out, w_final):
    count = lax.axis_size("seq")
    index = lax.axis_index("seq")
    half = index // (count // 2)
    positions = latent.shape[1] // CHAN
    span = positions // count
    latent_rows = latent.reshape(count, span, CHAN)
    latent_pos = lax.all_to_all(
        latent.reshape(1, count, span, CHAN), "seq", split_axis=1, concat_axis=0, tiled=True
    )
    qkv_flat, out_flat = gather_weights(w_qkv.T, w_attn_out.T)

    start = jnp.dot(latent_rows.reshape(positions, CHAN), w_in, preferred_element_type=jnp.float32)
    mods = lax.dynamic_index_in_dim(modulation, half, 0, keepdims=False)
    hidden = (normalize(start) * (1.0 + mods[1]) + mods[0]).astype(jnp.bfloat16)
    words = lax.dynamic_index_in_dim(text_embed, half, 0, keepdims=False)
    valid = lax.dynamic_index_in_dim(text_mask, half, 0, keepdims=False) > 0
    rows = jnp.concatenate([hidden, words], axis=0)

    cond_side = (jnp.arange(count) < count // 2)[:, None, None]
    frame_mods = jnp.where(cond_side, modulation[0][None], modulation[1][None])
    start_here = jnp.dot(
        latent_pos.reshape(positions, CHAN), w_in, preferred_element_type=jnp.float32
    ).reshape(count, span, -1)
    hidden_here = (
        normalize(start_here) * (1.0 + frame_mods[:, 1][:, None, :]) + frame_mods[:, 0][:, None, :]
    ).astype(jnp.bfloat16).reshape(positions, -1)

    swide, twide = SHEADS * HDIM, THEADS * HDIM
    spatial = [
        multiply(rows if i else hidden, qkv_flat, i * HEADS * HDIM, swide)
        .astype(jnp.bfloat16)
        for i in range(3)
    ]
    live = jnp.concatenate([jnp.ones((positions,), jnp.int32), valid.astype(jnp.int32)])[None]
    spatial_out = attend(spatial[0], spatial[1], spatial[2], live)
    spatial_pos = lax.all_to_all(
        spatial_out.reshape(1, count, span, swide), "seq", split_axis=1, concat_axis=0, tiled=True
    )
    temporal = [
        multiply(hidden_here, qkv_flat, (i * HEADS + SHEADS) * HDIM, twide)
        .astype(jnp.bfloat16)
        .reshape(count, span, twide)
        for i in range(3)
    ]
    temporal_pos = temporal_mix(*temporal)
    joined = jnp.concatenate(
        [spatial_pos.reshape(positions, swide), temporal_pos.reshape(positions, twide)], axis=1
    )
    mixed_out = multiply(joined, out_flat, 0, out_flat.shape[0])
    block = start_here + frame_mods[:, 2][:, None, :] * mixed_out.reshape(count, span, -1)
    final = (
        normalize(block) * (1.0 + frame_mods[:, 4][:, None, :]) + frame_mods[:, 3][:, None, :]
    ).astype(jnp.bfloat16)
    pred = jnp.dot(
        final.reshape(positions, -1), w_final, preferred_element_type=jnp.float32
    ).astype(jnp.bfloat16)
    pred = lax.optimization_barrier(pred).astype(jnp.float32).reshape(count, span, CHAN)
    cond_pred = pred[: count // 2]
    uncond_pred = pred[count // 2 :]
    guided_here = uncond_pred + GUIDE * (cond_pred - uncond_pred)
    both_halves = jnp.concatenate([guided_here, guided_here], axis=0)
    result = lax.all_to_all(
        both_halves.astype(jnp.bfloat16), "seq", split_axis=0, concat_axis=1, tiled=True
    ).astype(both_halves.dtype)
    return result.reshape(1, positions * CHAN)


def solution(mesh):
    in_specs = (
        P(("groups", "seq"), None),
        P("groups", None, None),
        P("groups", None),
        P("groups", None, None),
        P(),
        P(None, "seq"),
        P(None, "seq"),
        P(),
    )
    out_specs = P(("groups", "seq"), None)
    return jax.shard_map(
        per_device, mesh=mesh, in_specs=in_specs, out_specs=out_specs, check_vma=False
    )
```

```python
import functools

import jax
import jax.numpy as jnp
from jax import lax
from jax.experimental import pallas as pl
from jax.experimental.pallas import tpu as pltpu
from jax.sharding import PartitionSpec as P

HDIM = 128
SHEADS = 6
THEADS = 6
CHAN = 64
HEADS = 12


EPS = 1e-06
GUIDE = 5.0


def normalize(values):
    center = values - jnp.mean(values, axis=-1, keepdims=True)
    spread = jnp.mean(center * center, axis=-1, keepdims=True)
    return center * lax.rsqrt(spread + EPS)


def attend_kernel(query, keys, values, live, out):
    rows = query.shape[0]
    block = min(128, rows)
    for first in range(0, rows, block):
        at = pl.ds(first, block)
        scores = lax.dot_general(
            query[at, :], keys[...], (((1,), (1,)), ((), ())), preferred_element_type=jnp.float32
        ) * HDIM ** (-0.5)
        scores = jnp.where(live[...] > 0, scores, -1e30)
        top = jnp.max(scores, axis=-1, keepdims=True)
        weights = jnp.exp(scores - top)
        total = jnp.sum(weights, axis=-1, keepdims=True)
        mixed = jnp.dot(
            weights.astype(jnp.bfloat16), values[...], preferred_element_type=jnp.float32
        )
        out[at, :] = (mixed / total).astype(jnp.bfloat16)


def attend(queries, query, keys, values, live):
    def column(rows):
        return pl.BlockSpec((rows, HDIM), lambda head: (0, head))

    return pl.pallas_call(
        attend_kernel,
        grid=(query.shape[1] // HDIM,),
        out_shape=jax.ShapeDtypeStruct((queries, query.shape[1]), jnp.bfloat16),
        in_specs=[
            column(queries),
            column(keys.shape[0]),
            column(keys.shape[0]),
            pl.BlockSpec(live.shape, lambda head: (0, 0)),
        ],
        out_specs=column(queries),
    )(query, keys, values, live)


def temporal_mix(query, keys, values):
    frames, span = query.shape[0], query.shape[1]
    halved = (2, frames // 2, span, THEADS, HDIM)
    query, keys, values = (x.reshape(halved) for x in (query, keys, values))
    scores = jnp.einsum(
        "afpne,agpne->apnfg", query, keys, preferred_element_type=jnp.float32
    ) * HDIM ** (-0.5)
    top = jnp.max(scores, axis=-1, keepdims=True)
    weights = jnp.exp(scores - top)
    total = jnp.sum(weights, axis=-1)
    probs = weights.astype(jnp.bfloat16)
    mixed = jnp.einsum("apnfg,agpne->afpne", probs, values, preferred_element_type=jnp.float32)
    mixed = mixed / jnp.moveaxis(total, 3, 1)[..., None]
    return mixed.astype(jnp.bfloat16).reshape(frames, span, THEADS * HDIM)


def load_list(weights):
    loads = []
    for which, weight in enumerate(weights):
        third = weight.shape[0] // 3
        cuts = max(c for c in (1, 2) if third % (16 * c) == 0)
        loads += [(cut / cuts, which, cut, third // cuts) for cut in range(cuts)]
    return [load[1:] for load in sorted(loads)]


def gather_kernel(count, number, *refs):
    weights, wholes = refs[:number], refs[number : 2 * number]
    own_sem, ring_send, ring_recv, x_send, x_recv, core_send, core_recv = refs[2 * number :]
    chips = count // 2
    team, me = lax.axis_index("groups"), lax.axis_index("seq")
    core, chip = me % 2, me // 2
    place = (1 - chip % 2) * (chip // 2) + (chip % 2) * (chips - 1 - chip // 2)
    right_third, left_third = 2 * (team % 2), 1
    x_third = 2 - right_third
    parts = (right_third, left_third, x_third)

    def shard(spot, lane):
        spot = (spot + 2 * chips) % chips
        late = spot // (chips // 2)
        return 2 * ((1 - late) * 2 * spot + late * (2 * (chips - 1 - spot) + 1)) + lane

    loads = load_list(weights)

    def rows(item, part):
        which, cut, extent = loads[item]
        third = weights[which].shape[0] // 3
        return pl.ds(pl.multiple_of(part * third + cut * extent, extent), extent)

    def whole(item):
        return wholes[loads[item][0]]

    right, left = {"seq": shard(place + 1, core)}, {"seq": shard(place - 1, core)}
    sibling = {"seq": chip * 2 + 1 - core}
    across = {"groups": team + 1 - 2 * (team % 2)}

    barrier = pltpu.get_barrier_semaphore()
    for peer in (right, left, sibling, across):
        pl.semaphore_signal(barrier, inc=1, device_id=peer, device_id_type=pl.DeviceIdType.MESH)
    pl.semaphore_wait(barrier, 4)

    def remote(src, dst, send, recv, peer):
        return pltpu.make_async_remote_copy(
            src_ref=src,
            dst_ref=dst,
            send_sem=send,
            recv_sem=recv,
            device_id=peer,
            device_id_type=pl.DeviceIdType.MESH,
        )

    def ring(item, way, step, sending):
        toward = (1, -1)[way]
        spot = place - toward * step if sending else place - toward * (step + 1)
        view = whole(item).at[shard(spot, core), rows(item, parts[way])]
        src = weights[loads[item][0]].at[rows(item, parts[way])] if sending and step == 0 else view
        at = (item, way, step)
        return remote(src, view, ring_send.at[at], ring_recv.at[at], (right, left)[way])

    def cross(item, step, sending):
        part = right_third if sending else x_third
        view = whole(item).at[shard(place - step - 1, core), rows(item, part)]
        return remote(view, view, x_send.at[item, step], x_recv.at[item, step], across)

    def twin(item, kind, step, sending):
        spot = (place - step - 1, place + step + 1, place - step - 1)[kind]
        lane = core if sending else 1 - core
        view = whole(item).at[shard(spot, lane), rows(item, parts[kind])]
        at = (item, kind, step)
        return remote(view, view, core_send.at[at], core_recv.at[at], sibling)

    def lend(item, whose):
        view = wholes[item].at[whose]
        return remote(weights[item], view, own_sem.at[item, 1], own_sem.at[item, 2], sibling)

    items = range(len(loads))
    steps = chips - 1
    own = [pltpu.make_async_copy(weights[i], wholes[i].at[me], own_sem.at[i, 0]) for i in range(number)]
    for item in items:
        for way in range(2):
            ring(item, way, 0, True).start()
    for item in range(number):
        own[item].start()
        lend(item, me).start()
    for step in range(steps):
        for item in items:
            for way in range(2):
                ring(item, way, step, False).wait_recv()
                if step + 1 < steps:
                    ring(item, way, step + 1, True).start()
                if way == 0:
                    cross(item, step, True).start()
                twin(item, way, step, True).start()
            if step:
                cross(item, step - 1, False).wait_recv()
                twin(item, 2, step - 1, True).start()
    for item in items:
        cross(item, steps - 1, False).wait_recv()
        twin(item, 2, steps - 1, True).start()
    for item in items:
        for step in range(steps):
            for way in range(2):
                ring(item, way, step, True).wait_send()
            cross(item, step, True).wait_send()
            for kind in range(3):
                twin(item, kind, step, True).wait_send()
                twin(item, kind, step, False).wait_recv()
    for item in range(number):
        own[item].wait()
        lend(item, me).wait_send()
        lend(item, chip * 2 + 1 - core).wait_recv()


def gather_weights(*weights):
    count = lax.axis_size("seq")
    number, steps, loads = len(weights), count // 2 - 1, len(load_list(weights))
    wholes = pl.pallas_call(
        functools.partial(gather_kernel, count, number),
        out_shape=[jax.ShapeDtypeStruct((count,) + w.shape, w.dtype) for w in weights],
        in_specs=[pl.BlockSpec(memory_space=pl.ANY)] * number,
        out_specs=[pl.BlockSpec(memory_space=pl.ANY)] * number,
        scratch_shapes=[
            pltpu.SemaphoreType.DMA((number, 3)),
            pltpu.SemaphoreType.DMA((loads, 2, steps)),
            pltpu.SemaphoreType.DMA((loads, 2, steps)),
            pltpu.SemaphoreType.DMA((loads, steps)),
            pltpu.SemaphoreType.DMA((loads, steps)),
            pltpu.SemaphoreType.DMA((loads, 3, steps)),
            pltpu.SemaphoreType.DMA((loads, 3, steps)),
        ],
        compiler_params=pltpu.CompilerParams(collective_id=0, has_side_effects=True),
    )(*weights)
    return [x.reshape(count * w.shape[0], w.shape[1]) for x, w in zip(wholes, weights)]


def multiply(rows, flat, first, width):
    return lax.dot_general(
        rows,
        flat[first : first + width],
        (((1,), (1,)), ((), ())),
        preferred_element_type=jnp.float32,
    )


def per_device(latent, text_embed, text_mask, modulation, w_in, w_qkv, w_attn_out, w_final):
    count = lax.axis_size("seq")
    index = lax.axis_index("seq")
    half = index // (count // 2)
    positions = latent.shape[1] // CHAN
    span = positions // count
    latent_rows = latent.reshape(count, span, CHAN)
    latent_pos = lax.all_to_all(
        latent.reshape(1, count, span, CHAN), "seq", split_axis=1, concat_axis=0, tiled=True
    )
    qkv_flat, out_flat = gather_weights(w_qkv.T, w_attn_out.T)

    start = jnp.dot(latent_rows.reshape(positions, CHAN), w_in, preferred_element_type=jnp.float32)
    mods = lax.dynamic_index_in_dim(modulation, half, 0, keepdims=False)
    hidden = (normalize(start) * (1.0 + mods[1]) + mods[0]).astype(jnp.bfloat16)
    words = lax.dynamic_index_in_dim(text_embed, half, 0, keepdims=False)
    valid = lax.dynamic_index_in_dim(text_mask, half, 0, keepdims=False) > 0
    rows = jnp.concatenate([hidden, words], axis=0)

    cond_side = (jnp.arange(count) < count // 2)[:, None, None]
    frame_mods = jnp.where(cond_side, modulation[0][None], modulation[1][None])
    start_here = jnp.dot(
        latent_pos.reshape(positions, CHAN), w_in, preferred_element_type=jnp.float32
    ).reshape(count, span, -1)
    hidden_here = (
        normalize(start_here) * (1.0 + frame_mods[:, 1][:, None, :]) + frame_mods[:, 0][:, None, :]
    ).astype(jnp.bfloat16).reshape(positions, -1)

    swide, twide = SHEADS * HDIM, THEADS * HDIM
    spatial = [
        multiply(rows, qkv_flat, i * HEADS * HDIM, swide)
        .astype(jnp.bfloat16)
        for i in range(3)
    ]
    live = jnp.concatenate([jnp.ones((positions,), jnp.int32), valid.astype(jnp.int32)])[None]
    spatial_out = attend(positions, spatial[0], spatial[1], spatial[2], live)
    spatial_pos = lax.all_to_all(
        spatial_out.reshape(1, count, span, swide), "seq", split_axis=1, concat_axis=0, tiled=True
    )
    temporal = [
        multiply(hidden_here, qkv_flat, (i * HEADS + SHEADS) * HDIM, twide)
        .astype(jnp.bfloat16)
        .reshape(count, span, twide)
        for i in range(3)
    ]
    temporal_pos = temporal_mix(*temporal)
    joined = jnp.concatenate(
        [spatial_pos.reshape(positions, swide), temporal_pos.reshape(positions, twide)], axis=1
    )
    mixed_out = multiply(joined, out_flat, 0, out_flat.shape[0])
    block = start_here + frame_mods[:, 2][:, None, :] * mixed_out.reshape(count, span, -1)
    final = (
        normalize(block) * (1.0 + frame_mods[:, 4][:, None, :]) + frame_mods[:, 3][:, None, :]
    ).astype(jnp.bfloat16)
    pred = jnp.dot(
        final.reshape(positions, -1), w_final, preferred_element_type=jnp.float32
    ).astype(jnp.bfloat16)
    pred = lax.optimization_barrier(pred).astype(jnp.float32).reshape(count, span, CHAN)
    cond_pred = pred[: count // 2]
    uncond_pred = pred[count // 2 :]
    guided_here = uncond_pred + GUIDE * (cond_pred - uncond_pred)
    both_halves = jnp.concatenate([guided_here, guided_here], axis=0)
    result = lax.all_to_all(
        both_halves.astype(jnp.bfloat16), "seq", split_axis=0, concat_axis=1, tiled=True
    ).astype(both_halves.dtype)
    return result.reshape(1, positions * CHAN)


def solution(mesh):
    in_specs = (
        P(("groups", "seq"), None),
        P("groups", None, None),
        P("groups", None),
        P("groups", None, None),
        P(),
        P(None, "seq"),
        P(None, "seq"),
        P(),
    )
    out_specs = P(("groups", "seq"), None)
    return jax.shard_map(
        per_device, mesh=mesh, in_specs=in_specs, out_specs=out_specs, check_vma=False
    )
```
